32 devices in a mesh: seq: 4 (over x, core), ctx: 4 (over z), fsdp: 2 (over y).
Axes of the slice: x: 2, y: 2, z: 4, core: 2. Of those that a mesh axis runs over, the one named last changes fastest.
Arguments:
- hidden_in: bfloat16 [8, 512, 768], P(('seq', 'fsdp'), 'ctx'), may hold values from -6 to 6
- encoder_states: bfloat16 [8, 64, 768], P(('seq', 'fsdp'), 'ctx'), may hold values from -6 to 6
- out_grad: bfloat16 [8, 512, 768], P(('seq', 'fsdp'), 'ctx'), may hold values from -6 to 6
- bucket_index: int32 [512], replicated, may hold values from 0 to 31, as said below
- bias_table: float32 [32, 12], replicated, may hold values from -5 to 5
- self_gain: bfloat16 [768], P(('ctx', 'fsdp')), may hold values from 0.099609375 to 1.8984375
- self_query: bfloat16 [768, 768], P(('ctx', 'fsdp')), may hold values from -0.02734375 to 0.02734375
- self_key: bfloat16 [768, 768], P(('ctx', 'fsdp')), may hold values from -0.21875 to 0.21875
- self_value: bfloat16 [768, 768], P(('ctx', 'fsdp')), may hold values from -0.21875 to 0.21875
- self_output: bfloat16 [768, 768], P(('ctx', 'fsdp')), may hold values from -1.5 to 1.5
- cross_gain: bfloat16 [768], P(('ctx', 'fsdp')), may hold values from 0.099609375 to 1.8984375
- cross_query: bfloat16 [768, 768], P(('ctx', 'fsdp')), may hold values from -0.02734375 to 0.02734375
- cross_key: bfloat16 [768, 768], P(('ctx', 'fsdp')), may hold values from -0.21875 to 0.21875
- cross_value: bfloat16 [768, 768], P(('ctx', 'fsdp')), may hold values from -0.21875 to 0.21875
- cross_output: bfloat16 [768, 768], P(('ctx', 'fsdp')), may hold values from -1.5 to 1.5
- feed_gain: bfloat16 [768], P(('ctx', 'fsdp')), may hold values from 0.099609375 to 1.8984375
- gate_weight: bfloat16 [768, 2048], P(('ctx', 'fsdp')), may hold values from -0.21875 to 0.21875
- linear_weight: bfloat16 [768, 2048], P(('ctx', 'fsdp')), may hold values from -0.21875 to 0.21875
- down_weight: bfloat16 [2048, 768], P(('ctx', 'fsdp')), may hold values from -0.125 to 0.125
Outputs:
- layer_out: bfloat16 [8, 512, 768], P(('seq', 'fsdp'), 'ctx')
- input_grad: float32 [8, 512, 768], P(('seq', 'fsdp'), 'ctx')
- encoder_grad: float32 [8, 64, 768], P(('seq', 'fsdp'), 'ctx')
- grad_bias_table: float32 [32, 12], replicated
- grad_self_gain: float32 [768], P(('ctx', 'fsdp'))
- grad_self_query: float32 [768, 768], P(('ctx', 'fsdp'))
- grad_self_key: float32 [768, 768], P(('ctx', 'fsdp'))
- grad_self_value: float32 [768, 768], P(('ctx', 'fsdp'))
- grad_self_output: float32 [768, 768], P(('ctx', 'fsdp'))
- grad_cross_gain: float32 [768], P(('ctx', 'fsdp'))
- grad_cross_query: float32 [768, 768], P(('ctx', 'fsdp'))
- grad_cross_key: float32 [768, 768], P(('ctx', 'fsdp'))
- grad_cross_value: float32 [768, 768], P(('ctx', 'fsdp'))
- grad_cross_output: float32 [768, 768], P(('ctx', 'fsdp'))
- grad_feed_gain: float32 [768], P(('ctx', 'fsdp'))
- grad_gate_weight: float32 [768, 2048], P(('ctx', 'fsdp'))
- grad_linear_weight: float32 [768, 2048], P(('ctx', 'fsdp'))
- grad_down_weight: float32 [2048, 768], P(('ctx', 'fsdp'))
The draws below stay inside these ranges and needn't reach their ends.
Inputs may be any that keep to these rules, and one draw needn't show every extreme that they name: bucket_index[d] is the bucket of a key that lies d positions before its query; it is 0 at d = 0 and never falls as d grows.
All inputs are finite; a program needn't handle non-finite values.
Results may differ from the reference program's by a relative error of at most 0.025.
Values may be sent and summed in bfloat16 or wider, within the bound.
A program may use at most 256 MiB of HBM per device.

```python
import math
import jax
import jax.numpy as jnp
from jax import lax

D = 768
HEADS = 12
FF = 2048
BUCKETS = 32
HEAD = 64
LEN = 512
ENC = 64
SEQS = 8


def draw_bucket_index(key, part):
    source = jax.random.fold_in(key, 5303)
    increments = jax.random.randint(source, (LEN - 1,), 0, 3).astype(jnp.int32)
    running = jnp.concatenate([jnp.zeros((1,), jnp.int32), jnp.cumsum(increments).astype(jnp.int32)])
    capped = jnp.minimum(running, BUCKETS - 1).astype(jnp.int32)
    distance = jnp.arange(LEN, dtype=jnp.int32)
    return jnp.where(distance == LEN - 1, BUCKETS - 1, capped).astype(jnp.int32)


def level_of(own_key, extent, shards, least, high):
    factor_of = 1.0
    for axis_at, blocks in shards:
        heights = jax.random.uniform(jax.random.fold_in(jax.random.fold_in(own_key, 6), axis_at), (blocks,), jnp.float32, least / len(shards), high / len(shards))
        factor_of = factor_of * jnp.repeat(jnp.exp(heights), extent[axis_at] // blocks).reshape((-1,) + (1,) * (len(extent) - 1 - axis_at))
    return factor_of


def gaussian(own_key, dims, deviation, reach, split=(), kind=jnp.bfloat16):
    factor_of = level_of(own_key, dims, split, -0.22, 0.18) if split else 1.0
    drawn = jax.random.normal(own_key, dims, jnp.float32) * deviation * factor_of
    return jnp.minimum(jnp.maximum(drawn, -reach), reach).astype(kind)


def setup_inputs(seed: int = 0) -> dict:
    splits = jax.random.split(jax.random.key(seed), 20)
    return {
        "hidden_in": gaussian(splits[0], (SEQS, LEN, D), 1.0, 6.0, ((0, 8), (1, 4))),
        "encoder_states": gaussian(splits[1], (SEQS, ENC, D), 1.0, 6.0, ((0, 8), (1, 4))),
        "out_grad": gaussian(splits[2], (SEQS, LEN, D), 1.0, 6.0, ((0, 8), (1, 4))),
        "bucket_index": draw_bucket_index(jax.random.fold_in(splits[19], 71), 0),
        "bias_table": gaussian(splits[4], (BUCKETS, HEADS), 1.0, 5.0, (), jnp.float32),
        "self_gain": jnp.clip(1.0 + 0.18 * jax.random.normal(splits[5], (D,), jnp.float32), 0.099609375, 1.8984375).astype(jnp.bfloat16),
        "self_query": gaussian(splits[6], (D, D), (D * HEAD) ** -0.5, 0.02734375, ((0, 8),)),
        "self_key": gaussian(splits[7], (D, D), D ** -0.5, 0.21875, ((0, 8),)),
        "self_value": gaussian(splits[8], (D, D), D ** -0.5, 0.21875, ((0, 8),)),
        "self_output": gaussian(splits[9], (D, D), 16 ** -0.5, 1.5, ((0, 8),)),
        "cross_gain": jnp.clip(1.0 + 0.18 * jax.random.normal(splits[10], (D,), jnp.float32), 0.099609375, 1.8984375).astype(jnp.bfloat16),
        "cross_query": gaussian(splits[11], (D, D), (D * HEAD) ** -0.5, 0.02734375, ((0, 8),)),
        "cross_key": gaussian(splits[12], (D, D), D ** -0.5, 0.21875, ((0, 8),)),
        "cross_value": gaussian(splits[13], (D, D), D ** -0.5, 0.21875, ((0, 8),)),
        "cross_output": gaussian(splits[14], (D, D), 16 ** -0.5, 1.5, ((0, 8),)),
        "feed_gain": jnp.clip(1.0 + 0.18 * jax.random.normal(splits[15], (D,), jnp.float32), 0.099609375, 1.8984375).astype(jnp.bfloat16),
        "gate_weight": gaussian(splits[16], (D, FF), D ** -0.5, 0.21875, ((0, 8),)),
        "linear_weight": gaussian(splits[17], (D, FF), D ** -0.5, 0.21875, ((0, 8),)),
        "down_weight": gaussian(splits[18], (FF, D), FF ** -0.5, 0.125, ((0, 8),)),
    }


EPSILON = 1e-06
NEGATIVE = -1e+30
HIGHEST = lax.Precision.HIGHEST

def to_bf16(values):
    return lax.optimization_barrier(values.astype(jnp.bfloat16))

def product(left, right):
    return jnp.dot(left, right, preferred_element_type=jnp.float32)

def row_contract(left, right):
    return jnp.dot(left.T, right, preferred_element_type=jnp.float32)

def col_contract(left, right):
    return jnp.dot(left, right.T, preferred_element_type=jnp.float32)

def norm_forward(values, gain):
    inverse = lax.rsqrt(lax.optimization_barrier(jnp.mean(values * values, axis=-1, keepdims=True)) + EPSILON)
    normed = values * inverse
    return (to_bf16(normed * gain.astype(jnp.float32)), normed, inverse)

def norm_backward(upstream, normed, inverse, gain):
    grad_gain = lax.optimization_barrier(jnp.sum(upstream * normed, axis=0))
    grad_normed = upstream * gain.astype(jnp.float32)
    grad_values = inverse * (grad_normed - normed * lax.optimization_barrier(jnp.mean(grad_normed * normed, axis=-1, keepdims=True)))
    return (grad_values, grad_gain)

def geglu(gate_pre, linear_pre):
    return jax.nn.gelu(gate_pre, approximate=True) * linear_pre

def split_heads(values):
    return values.astype(jnp.float32).reshape(values.shape[0], HEADS, HEAD)

def attend_forward(query, keys, values, extra, allowed):
    scores = jnp.einsum('qhe,khe->hqk', split_heads(query), split_heads(keys)) + extra
    scores = jnp.where(allowed, scores, NEGATIVE)
    top = lax.optimization_barrier(jnp.max(scores, axis=-1, keepdims=True))
    weights = jnp.where(allowed, jnp.exp(scores - top), 0.0)
    total = lax.optimization_barrier(jnp.sum(weights, axis=-1, keepdims=True))
    mixed = jnp.einsum('hqk,khe->qhe', to_bf16(weights).astype(jnp.float32), split_heads(values))
    result = to_bf16((mixed / jnp.transpose(total, (1, 0, 2))).reshape(query.shape[0], D))
    return (result, (top + jnp.log(total))[:, :, 0])

def attend_backward(query, keys, values, extra, allowed, lse, output, grad_output):
    split_grad = split_heads(grad_output)
    delta = lax.optimization_barrier(jnp.sum(split_grad * split_heads(output), axis=-1)).T
    scores = jnp.einsum('qhe,khe->hqk', split_heads(query), split_heads(keys)) + extra
    scores = jnp.where(allowed, scores, NEGATIVE)
    probs = jnp.where(allowed, jnp.exp(scores - lse[:, :, None]), 0.0)
    grad_probs = jnp.einsum('qhe,khe->hqk', split_grad, split_heads(values))
    grad_scores = probs * (grad_probs - delta[:, :, None])
    rounded = to_bf16(grad_scores).astype(jnp.float32)
    grad_query = jnp.einsum('hqk,khe->qhe', rounded, split_heads(keys)).reshape(query.shape[0], D)
    grad_keys = jnp.einsum('hqk,qhe->khe', rounded, split_heads(query)).reshape(keys.shape[0], D)
    grad_values = jnp.einsum('hqk,qhe->khe', to_bf16(probs).astype(jnp.float32), split_grad).reshape(keys.shape[0], D)
    return (grad_query, grad_keys, grad_values, grad_scores)

def sequence_pass(hidden_row, encoder_row, grad_row, params, bias_dist):
    self_gain, self_query, self_key, self_value, self_output, cross_gain, cross_query, cross_key, cross_value, cross_output, feed_gain, gate_weight, linear_weight, down_weight = params
    block_size = math.gcd(LEN, 512)
    block_count = LEN // block_size
    positions = jnp.arange(LEN, dtype=jnp.int32)
    numbers = jnp.arange(block_count, dtype=jnp.int32)

    def self_layout(number):
        offset = (number * block_size + jnp.arange(block_size, dtype=jnp.int32))[:, None] - positions[None, :]
        distance = jnp.clip(offset, 0, LEN - 1)
        return (jnp.take(bias_dist, distance, axis=1), (offset >= 0)[None], distance)

    def rows_of(values, number):
        return lax.dynamic_slice_in_dim(values, number * block_size, block_size, 0)
    start_x = hidden_row.astype(jnp.float32)
    norm_one, normed_one, inverse_one = norm_forward(start_x, self_gain)
    query = to_bf16(product(norm_one, self_query))
    keys = to_bf16(product(norm_one, self_key))
    values = to_bf16(product(norm_one, self_value))

    def self_forward(carried, number):
        extra, allowed, distance = self_layout(number)
        return (carried, attend_forward(rows_of(query, number), keys, values, extra, allowed))
    _, (attn, self_lse) = lax.scan(self_forward, None, numbers)
    attn = attn.reshape(LEN, D)
    after_self = start_x + product(attn, self_output)
    norm_two, normed_two, inverse_two = norm_forward(after_self, cross_gain)
    cross_q = to_bf16(product(norm_two, cross_query))
    cross_keys = to_bf16(product(encoder_row, cross_key))
    cross_values = to_bf16(product(encoder_row, cross_value))

    def cross_forward(carried, number):
        return (carried, attend_forward(rows_of(cross_q, number), cross_keys, cross_values, 0.0, True))
    _, (cattn, cross_lse) = lax.scan(cross_forward, None, numbers)
    cattn = cattn.reshape(LEN, D)
    after_cross = after_self + product(cattn, cross_output)
    norm_three, normed_three, inverse_three = norm_forward(after_cross, feed_gain)
    gate_pre = product(norm_three, gate_weight)
    linear_pre = product(norm_three, linear_weight)
    middle = to_bf16(geglu(gate_pre, linear_pre))
    layer_row = (after_cross + product(middle, down_weight)).astype(jnp.bfloat16)
    grad_down = row_contract(middle, grad_row)
    grad_middle = col_contract(grad_row, down_weight)
    _, pull_back = jax.vjp(geglu, gate_pre, linear_pre)
    grad_gate_pre, grad_linear_pre = pull_back(grad_middle)
    gate_round = to_bf16(grad_gate_pre)
    linear_round = to_bf16(grad_linear_pre)
    grad_gate = row_contract(norm_three, gate_round)
    grad_linear = row_contract(norm_three, linear_round)
    back_three, grad_feed_gain = norm_backward(col_contract(gate_round, gate_weight) + col_contract(linear_round, linear_weight), normed_three, inverse_three, feed_gain)
    grad_after_cross = grad_row.astype(jnp.float32) + back_three
    cross_round = to_bf16(grad_after_cross)
    grad_cross_output = row_contract(cattn, cross_round)
    grad_cattn = to_bf16(col_contract(cross_round, cross_output))

    def cross_backward(carried, number):
        grad_query, grad_keys, grad_values, _ = attend_backward(rows_of(cross_q, number), cross_keys, cross_values, 0.0, True, cross_lse[number], rows_of(cattn, number), rows_of(grad_cattn, number))
        return ((carried[0] + grad_keys, carried[1] + grad_values), grad_query)
    empty_enc = jnp.zeros((ENC, D), jnp.float32)
    (cross_key_sum, cross_value_sum), grad_cq = lax.scan(cross_backward, (empty_enc, empty_enc), numbers)
    grad_cq = to_bf16(grad_cq.reshape(LEN, D))
    cross_key_round = to_bf16(cross_key_sum)
    cross_value_round = to_bf16(cross_value_sum)
    grad_cross_query = row_contract(norm_two, grad_cq)
    grad_cross_key = row_contract(encoder_row, cross_key_round)
    grad_cross_value = row_contract(encoder_row, cross_value_round)
    encoder_grad_row = col_contract(cross_key_round, cross_key) + col_contract(cross_value_round, cross_value)
    back_two, grad_cross_gain = norm_backward(col_contract(grad_cq, cross_query), normed_two, inverse_two, cross_gain)
    grad_after_self = grad_after_cross + back_two
    self_round = to_bf16(grad_after_self)
    grad_self_output = row_contract(attn, self_round)
    grad_attn = to_bf16(col_contract(self_round, self_output))

    def self_backward(carried, number):
        extra, allowed, distance = self_layout(number)
        grad_query, grad_keys, grad_values, grad_scores = attend_backward(rows_of(query, number), keys, values, extra, allowed, self_lse[number], rows_of(attn, number), rows_of(grad_attn, number))
        grad_dist = jax.ops.segment_sum(grad_scores.reshape(HEADS, -1).T, distance.reshape(-1), num_segments=LEN)
        return ((carried[0] + grad_keys, carried[1] + grad_values, carried[2] + grad_dist), grad_query)
    empty_seq = jnp.zeros((LEN, D), jnp.float32)
    (key_sum, value_sum, dist_sum), grad_q = lax.scan(self_backward, (empty_seq, empty_seq, jnp.zeros((LEN, HEADS), jnp.float32)), numbers)
    grad_q = to_bf16(grad_q.reshape(LEN, D))
    grad_k = to_bf16(key_sum)
    grad_v = to_bf16(value_sum)
    grad_self_query = row_contract(norm_one, grad_q)
    grad_self_key = row_contract(norm_one, grad_k)
    grad_self_value = row_contract(norm_one, grad_v)
    upstream_one = col_contract(grad_q, self_query) + col_contract(grad_k, self_key) + col_contract(grad_v, self_value)
    back_one, grad_self_gain = norm_backward(upstream_one, normed_one, inverse_one, self_gain)
    input_row = grad_after_self + back_one
    grads = (grad_self_gain, grad_self_query, grad_self_key, grad_self_value, grad_self_output, grad_cross_gain, grad_cross_query, grad_cross_key, grad_cross_value, grad_cross_output, grad_feed_gain, grad_gate, grad_linear, grad_down)
    return (layer_row, input_row, encoder_grad_row, grads, dist_sum)

def reference(hidden_in, encoder_states, out_grad, bucket_index, bias_table, self_gain, self_query, self_key, self_value, self_output, cross_gain, cross_query, cross_key, cross_value, cross_output, feed_gain, gate_weight, linear_weight, down_weight):
    params = (self_gain, self_query, self_key, self_value, self_output, cross_gain, cross_query, cross_key, cross_value, cross_output, feed_gain, gate_weight, linear_weight, down_weight)
    onehot = (bucket_index[:, None] == jnp.arange(BUCKETS, dtype=jnp.int32)[None, :]).astype(jnp.float32)
    bias_dist = jnp.dot(onehot, bias_table, precision=HIGHEST).T
    empty_grads = tuple((jnp.zeros(member.shape, jnp.float32) for member in params))

    def per_sequence(totals, inputs):
        hidden_row, encoder_row, grad_row = inputs
        layer_row, input_row, encoder_grad_row, grads, dist_sum = sequence_pass(hidden_row, encoder_row, grad_row, params, bias_dist)
        sums = tuple((running_sum + new_grad for running_sum, new_grad in zip(totals[0], grads)))
        return ((sums, totals[1] + dist_sum), (layer_row, input_row, encoder_grad_row))
    (grads, grad_dist), (layer_out, input_grad, encoder_grad) = lax.scan(per_sequence, (empty_grads, jnp.zeros((LEN, HEADS), jnp.float32)), (hidden_in, encoder_states, out_grad))
    grad_table = jnp.dot(onehot.T, grad_dist, precision=HIGHEST)
    return (layer_out, input_grad, encoder_grad, grad_table, grads[0], grads[1], grads[2], grads[3], grads[4], grads[5], grads[6], grads[7], grads[8], grads[9], grads[10], grads[11], grads[12], grads[13])
```

```python
from functools import partial
import math

import jax
import jax.numpy as jnp
from jax import lax
from jax.sharding import PartitionSpec as P

EPSILON = 1e-06
NEGATIVE = -1e30
HIGHEST = lax.Precision.HIGHEST


LANES = 128


def fold_rows(rows, height):
    count = -(-rows.shape[-2] // height)
    short = count * height - rows.shape[-2]
    padding = [(0, 0)] * (rows.ndim - 2) + [(0, short), (0, 0)]
    padded = jnp.pad(rows, padding)
    return jnp.concatenate(
        [padded[..., number * height : (number + 1) * height, :] for number in range(count)],
        axis=-1,
    )


def unfold_rows(columns, row_count, features):
    count = columns.shape[-1] // features
    stacked = jnp.concatenate(
        [columns[..., number * features : (number + 1) * features] for number in range(count)],
        axis=-2,
    )
    return stacked[..., :row_count, :]


def gain_columns(gains, dtype):
    columns = jnp.stack([member.astype(dtype) for member in gains], axis=1)
    return jnp.pad(columns, ((0, 0), (0, LANES - columns.shape[1])))


def product(left, right):
    return jnp.dot(left, right, preferred_element_type=jnp.float32)


def row_contract(left, right):
    return lax.dot_general(
        left, right, (((0,), (0,)), ((), ())), preferred_element_type=jnp.float32
    )


def col_contract(left, right):
    return lax.dot_general(
        left, right, (((1,), (1,)), ((), ())), preferred_element_type=jnp.float32
    )


def norm_forward(values, gain):
    inverse = lax.rsqrt(jnp.mean(values * values, axis=-1, keepdims=True) + EPSILON)
    normed = values * inverse
    return ((normed * gain.astype(jnp.float32)).astype(jnp.bfloat16), normed, inverse)


def norm_backward(upstream, normed, inverse, gain):
    grad_gain = jnp.sum(upstream * normed, axis=0)
    grad_normed = upstream * gain.astype(jnp.float32)
    grad_values = inverse * (
        grad_normed - normed * jnp.mean(grad_normed * normed, axis=-1, keepdims=True)
    )
    return (grad_values, grad_gain)


def geglu(gate_pre, linear_pre):
    return jax.nn.gelu(gate_pre, approximate=True) * linear_pre


def by_heads(values, head_count):
    return values.reshape(values.shape[0], head_count, values.shape[1] // head_count)


def band_onehot(bucket_rev, buckets, query_rows, key_rows, query_first, key_first):
    length = bucket_rev.shape[0] // 2
    offset_first = query_first - key_first
    upper_band = lax.dynamic_slice_in_dim(bucket_rev, length - 1 - offset_first, key_rows, 0)
    lower_band = lax.dynamic_slice_in_dim(
        bucket_rev, length - offset_first - query_rows, query_rows - 1, 0
    )
    slots = jnp.concatenate([upper_band, jnp.full((1,), -1, jnp.int32), lower_band])
    return (slots[:, None] == jnp.arange(buckets, dtype=jnp.int32)[None, :]).astype(jnp.float32)


def spread_band(band, query_rows, key_rows):
    head_count, width = band.shape
    tiled = jnp.broadcast_to(band[:, None, :], (head_count, query_rows, width)).reshape(
        head_count, query_rows * width
    )
    return tiled[:, : query_rows * (width - 1)].reshape(head_count, query_rows, width - 1)[
        :, :, :key_rows
    ]


def fold_band(grad_scores, width):
    head_count, query_rows, key_rows = grad_scores.shape
    padded = jnp.pad(grad_scores, ((0, 0), (0, 0), (0, width - 1 - key_rows))).reshape(
        head_count, query_rows * (width - 1)
    )
    padded = jnp.pad(padded, ((0, 0), (0, query_rows)))
    return jnp.sum(padded.reshape(head_count, query_rows, width), axis=1)


def self_scores(query, key_block, query_first, key_first, bucket_rev, bias_table):
    head_count = bias_table.shape[1]
    query_rows = query.shape[0]
    key_rows = key_block.shape[0]
    scores = jnp.einsum(
        "qhe,khe->hqk",
        by_heads(query, head_count),
        by_heads(key_block, head_count),
        preferred_element_type=jnp.float32,
    )
    offset = (query_first + jnp.arange(query_rows, dtype=jnp.int32))[:, None] - (
        key_first + jnp.arange(key_rows, dtype=jnp.int32)
    )[None, :]
    allowed = offset >= 0
    onehot = band_onehot(
        bucket_rev, bias_table.shape[0], query_rows, key_rows, query_first, key_first
    )
    band = jnp.dot(onehot, bias_table, precision=HIGHEST).T
    scores = jnp.where(allowed[None], scores + spread_band(band, query_rows, key_rows), NEGATIVE)
    return (scores, allowed, onehot)


def table_terms(grad_scores, onehot):
    band_grad = fold_band(grad_scores, onehot.shape[0])
    return jnp.dot(onehot.T, band_grad.T, precision=HIGHEST)


def fold_blocks(block_step, running, arrays, first_row):
    piece_rows = arrays[0].shape[0]
    block_size = math.gcd(piece_rows, 512) if piece_rows > 512 else piece_rows
    if block_size == piece_rows:
        return block_step(running, arrays, first_row)
    block_count = piece_rows // block_size
    stacked = tuple(
        (member.reshape((block_count, block_size) + member.shape[1:]) for member in arrays)
    )

    def scan_block(state_now, scanned):
        number, blocks = scanned
        return (block_step(state_now, blocks, first_row + number * block_size), None)

    result, _ = lax.scan(scan_block, running, (jnp.arange(block_count, dtype=jnp.int32), stacked))
    return result


def forward_step(running, blocks, key_first, query, query_first, bucket_rev, bias_table):
    top, total, mixed = running
    key_block, value_block = blocks
    head_count = bias_table.shape[1]
    scores, allowed, _ = self_scores(
        query, key_block, query_first, key_first, bucket_rev, bias_table
    )
    new_top = jnp.maximum(top, jnp.max(scores, axis=-1))
    weights = jnp.where(allowed[None], jnp.exp(scores - new_top[:, :, None]), 0.0)
    rescale = jnp.exp(top - new_top)
    total = total * rescale + jnp.sum(weights, axis=-1)
    update = jnp.einsum(
        "hqk,khe->qhe",
        weights.astype(jnp.bfloat16),
        by_heads(value_block, head_count),
        preferred_element_type=jnp.float32,
    )
    mixed = mixed * rescale.T[:, :, None] + update
    return (new_top, total, mixed)


def backward_core(
    query,
    grad_attn,
    lse_rows,
    delta_rows,
    key_block,
    value_block,
    query_first,
    key_first,
    bucket_rev,
    bias_table,
):
    head_count = bias_table.shape[1]
    scores, allowed, onehot = self_scores(
        query, key_block, query_first, key_first, bucket_rev, bias_table
    )
    probs = jnp.where(allowed[None], jnp.exp(scores - lse_rows.T[:, :, None]), 0.0)
    grad_probs = jnp.einsum(
        "qhe,khe->hqk",
        by_heads(grad_attn, head_count),
        by_heads(value_block, head_count),
        preferred_element_type=jnp.float32,
    )
    grad_scores = probs * (grad_probs - delta_rows.T[:, :, None])
    return (probs, grad_scores, onehot)


def partial_step(
    running,
    blocks,
    key_first,
    query,
    grad_attn,
    lse_rows,
    delta_rows,
    query_first,
    bucket_rev,
    bias_table,
):
    grad_query, grad_keys, grad_values, table_part = running
    key_block, value_block = blocks
    head_count = bias_table.shape[1]
    probs, grad_scores, onehot = backward_core(
        query,
        grad_attn,
        lse_rows,
        delta_rows,
        key_block,
        value_block,
        query_first,
        key_first,
        bucket_rev,
        bias_table,
    )
    rounded = grad_scores.astype(jnp.bfloat16)
    grad_query = grad_query + jnp.einsum(
        "hqk,khe->qhe", rounded, by_heads(key_block, head_count), preferred_element_type=jnp.float32
    )
    key_part = jnp.einsum(
        "hqk,qhe->khe", rounded, by_heads(query, head_count), preferred_element_type=jnp.float32
    ).reshape(key_block.shape[0], -1)
    value_part = jnp.einsum(
        "hqk,qhe->khe",
        probs.astype(jnp.bfloat16),
        by_heads(grad_attn, head_count),
        preferred_element_type=jnp.float32,
    ).reshape(key_block.shape[0], -1)
    grad_keys = lax.dynamic_update_slice_in_dim(grad_keys, key_part, key_first, 0)
    grad_values = lax.dynamic_update_slice_in_dim(grad_values, value_part, key_first, 0)
    table_part = table_part + table_terms(grad_scores, onehot)
    return (grad_query, grad_keys, grad_values, table_part)


def plain_forward(query, keys, values, head_count):
    scores = jnp.einsum(
        "qhe,khe->hqk",
        by_heads(query, head_count),
        by_heads(keys, head_count),
        preferred_element_type=jnp.float32,
    )
    top = jnp.max(scores, axis=-1, keepdims=True)
    weights = jnp.exp(scores - top)
    total = jnp.sum(weights, axis=-1, keepdims=True)
    mixed = jnp.einsum(
        "hqk,khe->qhe",
        weights.astype(jnp.bfloat16),
        by_heads(values, head_count),
        preferred_element_type=jnp.float32,
    )
    result = (
        (mixed / jnp.transpose(total, (1, 0, 2))).reshape(query.shape[0], -1).astype(jnp.bfloat16)
    )
    return (result, (top + jnp.log(total))[:, :, 0])


def plain_backward(query, keys, values, lse, output, grad_output, head_count):
    split_grad = by_heads(grad_output, head_count)
    delta = jnp.sum(
        split_grad.astype(jnp.float32) * by_heads(output, head_count).astype(jnp.float32), axis=-1
    ).T
    scores = jnp.einsum(
        "qhe,khe->hqk",
        by_heads(query, head_count),
        by_heads(keys, head_count),
        preferred_element_type=jnp.float32,
    )
    probs = jnp.exp(scores - lse[:, :, None])
    grad_probs = jnp.einsum(
        "qhe,khe->hqk", split_grad, by_heads(values, head_count), preferred_element_type=jnp.float32
    )
    rounded = (probs * (grad_probs - delta[:, :, None])).astype(jnp.bfloat16)
    grad_query = jnp.einsum(
        "hqk,khe->qhe", rounded, by_heads(keys, head_count), preferred_element_type=jnp.float32
    ).reshape(query.shape[0], -1)
    grad_keys = jnp.einsum(
        "hqk,qhe->khe", rounded, by_heads(query, head_count), preferred_element_type=jnp.float32
    ).reshape(keys.shape[0], -1)
    grad_values = jnp.einsum(
        "hqk,qhe->khe", probs.astype(jnp.bfloat16), split_grad, preferred_element_type=jnp.float32
    ).reshape(keys.shape[0], -1)
    return (grad_query, grad_keys, grad_values)


def reduce_terms(terms):
    groups = lax.axis_size("seq")
    share = terms.shape[1] // groups
    stacked = jnp.stack(
        [terms[:, number * share : (number + 1) * share] for number in range(groups)]
    )
    part = lax.psum_scatter(stacked, "seq", scatter_dimension=0, tiled=False)
    part = lax.psum_scatter(part, ("ctx", "fsdp"), scatter_dimension=0, tiled=True)
    return join_columns(lax.all_gather(part, "seq", axis=0, tiled=False))


def join_columns(stacked):
    return jnp.concatenate([stacked[number] for number in range(stacked.shape[0])], axis=1)


def gather_pack(pack):
    share = pack.shape[1] // lax.axis_size("seq")
    own = lax.dynamic_slice_in_dim(pack, lax.axis_index("seq") * share, share, 1)
    rows = lax.all_gather(own, ("ctx", "fsdp"), axis=0, tiled=True)
    return join_columns(lax.all_gather(rows, "seq", axis=0, tiled=False))


def even_columns(members):
    joined = jnp.concatenate(members, axis=1)
    return jnp.pad(joined, ((0, 0), (0, -joined.shape[1] % (LANES * lax.axis_size("seq")))))


def per_device(
    hidden_in,
    encoder_states,
    out_grad,
    bucket_index,
    bias_table,
    self_gain,
    self_query,
    self_key,
    self_value,
    self_output,
    cross_gain,
    cross_query,
    cross_key,
    cross_value,
    cross_output,
    feed_gain,
    gate_weight,
    linear_weight,
    down_weight,
):
    shards = lax.axis_size(("ctx", "fsdp"))
    features = self_query.shape[1]
    hidden = gate_weight.shape[1]
    pack = even_columns(
        [
            self_query,
            self_key,
            self_value,
            self_output,
            cross_query,
            cross_key,
            cross_value,
            cross_output,
            gate_weight,
            linear_weight,
            fold_rows(down_weight, self_query.shape[0]),
            gain_columns((self_gain, cross_gain, feed_gain), jnp.bfloat16),
        ]
    )
    pack = gather_pack(pack)
    (
        self_query,
        self_key,
        self_value,
        self_output,
        cross_query,
        cross_key,
        cross_value,
        cross_output,
    ) = (pack[:, number * features : (number + 1) * features] for number in range(8))
    first = 8 * features
    gate_weight = pack[:, first : first + hidden]
    linear_weight = pack[:, first + hidden : first + 2 * hidden]
    first = first + 2 * hidden
    width = -(-(hidden // shards) // (features // shards)) * features
    down_weight = unfold_rows(
        pack[:, first : first + width].reshape(shards, -1, width), hidden // shards, features
    ).reshape(hidden, features)
    gains = pack[:, first + width : first + width + LANES].T
    self_gain, cross_gain, feed_gain = gains[0], gains[1], gains[2]
    tokens = hidden_in.shape[1]
    length = bucket_index.shape[0]
    head_count = bias_table.shape[1]
    buckets = bias_table.shape[0]
    query_first = lax.axis_index("ctx") * tokens
    bucket_rev = jnp.flip(jnp.concatenate([jnp.full((length,), -1, jnp.int32), bucket_index]))
    start_x = hidden_in[0].astype(jnp.float32)
    norm_one, normed_one, inverse_one = norm_forward(start_x, self_gain)
    projected = product(norm_one, pack[:, : 3 * features]).astype(jnp.bfloat16)
    query = projected[:, :features]
    encoder_local = encoder_states[0]
    cross_local = product(encoder_local, pack[:, 5 * features : 7 * features]).astype(jnp.bfloat16)
    encoder_rows = encoder_local.shape[0]
    blocks = lax.all_gather(
        jnp.concatenate([projected[:, features:], cross_local], axis=0), "ctx", axis=0, tiled=False
    )
    both = blocks[:, :tokens].reshape(length, 2 * features)
    keys, values = both[:, :features], both[:, features:]
    both = blocks[:, tokens:].reshape(-1, 2 * features)
    cross_keys, cross_values = both[:, :features], both[:, features:]
    empty_top = jnp.full((head_count, tokens), NEGATIVE, jnp.float32)
    empty_total = jnp.zeros((head_count, tokens), jnp.float32)
    empty_mixed = jnp.zeros((tokens, head_count, query.shape[1] // head_count), jnp.float32)
    forward_bound = partial(
        forward_step,
        query=query,
        query_first=query_first,
        bucket_rev=bucket_rev,
        bias_table=bias_table,
    )
    top, total, mixed = fold_blocks(
        forward_bound,
        (empty_top, empty_total, empty_mixed),
        (keys, values),
        jnp.int32(0),
    )
    attn = (mixed / total.T[:, :, None]).reshape(tokens, -1).astype(jnp.bfloat16)
    self_lse = (top + jnp.log(total)).T
    after_self = start_x + product(attn, self_output)
    norm_two, normed_two, inverse_two = norm_forward(after_self, cross_gain)
    cross_q = product(norm_two, cross_query).astype(jnp.bfloat16)
    cattn, cross_lse = plain_forward(cross_q, cross_keys, cross_values, head_count)
    after_cross = after_self + product(cattn, cross_output)
    norm_three, normed_three, inverse_three = norm_forward(after_cross, feed_gain)
    gate_pre = product(norm_three, gate_weight)
    linear_pre = product(norm_three, linear_weight)
    middle = geglu(gate_pre, linear_pre).astype(jnp.bfloat16)
    layer_out = (after_cross + product(middle, down_weight)).astype(jnp.bfloat16)
    grad_top = out_grad[0]
    grad_down = row_contract(middle, grad_top)
    grad_middle = col_contract(grad_top, down_weight)
    _, pull_back = jax.vjp(geglu, gate_pre, linear_pre)
    grad_gate_pre, grad_linear_pre = pull_back(grad_middle)
    gate_round = grad_gate_pre.astype(jnp.bfloat16)
    linear_round = grad_linear_pre.astype(jnp.bfloat16)
    grad_gate = row_contract(norm_three, gate_round)
    grad_linear = row_contract(norm_three, linear_round)
    back_three, grad_feed_gain = norm_backward(
        col_contract(gate_round, gate_weight) + col_contract(linear_round, linear_weight),
        normed_three,
        inverse_three,
        feed_gain,
    )
    grad_after_cross = grad_top.astype(jnp.float32) + back_three
    cross_round = grad_after_cross.astype(jnp.bfloat16)
    grad_cross_output = row_contract(cattn, cross_round)
    grad_cattn = col_contract(cross_round, cross_output).astype(jnp.bfloat16)
    grad_cq, cross_key_terms, cross_value_terms = plain_backward(
        cross_q, cross_keys, cross_values, cross_lse, cattn, grad_cattn, head_count
    )
    grad_cq = grad_cq.astype(jnp.bfloat16)
    grad_cross_query = row_contract(norm_two, grad_cq)
    back_two, grad_cross_gain = norm_backward(
        col_contract(grad_cq, cross_query), normed_two, inverse_two, cross_gain
    )
    grad_after_self = grad_after_cross + back_two
    self_round = grad_after_self.astype(jnp.bfloat16)
    grad_self_output = row_contract(attn, self_round)
    grad_attn = col_contract(self_round, self_output).astype(jnp.bfloat16)
    delta_rows = jnp.sum(
        by_heads(grad_attn, head_count).astype(jnp.float32)
        * by_heads(attn, head_count).astype(jnp.float32),
        axis=-1,
    )
    empty_rows = jnp.zeros((tokens, query.shape[1]), jnp.float32)
    empty_table = jnp.zeros((buckets, head_count), jnp.float32)
    partial_bound = partial(
        partial_step,
        query=query,
        grad_attn=grad_attn,
        lse_rows=self_lse,
        delta_rows=delta_rows,
        query_first=query_first,
        bucket_rev=bucket_rev,
        bias_table=bias_table,
    )
    empty_whole = jnp.zeros((length, query.shape[1]), jnp.float32)
    grad_query, key_terms, value_terms, table_part = fold_blocks(
        partial_bound,
        (empty_rows.reshape(tokens, head_count, -1), empty_whole, empty_whole, empty_table),
        (keys, values),
        jnp.int32(0),
    )
    terms = jnp.concatenate(
        [
            jnp.concatenate([key_terms, value_terms], axis=1).reshape(-1, tokens, 2 * features),
            jnp.concatenate([cross_key_terms, cross_value_terms], axis=1).reshape(
                -1, encoder_rows, 2 * features
            ),
        ],
        axis=1,
    ).astype(jnp.bfloat16)
    sums = lax.psum_scatter(terms, "ctx", scatter_dimension=0, tiled=False)
    cross_both = sums[tokens:]
    grad_cross_both = row_contract(encoder_local, cross_both)
    grad_cross_key, grad_cross_value = (
        grad_cross_both[:, :features],
        grad_cross_both[:, features:],
    )
    encoder_grad = col_contract(cross_both, pack[:, 5 * features : 7 * features])
    grad_q = grad_query.reshape(tokens, -1).astype(jnp.bfloat16)
    grad_projected = jnp.concatenate([grad_q, sums[:tokens]], axis=1)
    grad_self_projections = row_contract(norm_one, grad_projected)
    upstream_one = col_contract(grad_projected, pack[:, : 3 * features])
    back_one, grad_self_gain = norm_backward(upstream_one, normed_one, inverse_one, self_gain)
    input_grad = grad_after_self + back_one
    grad_table = lax.psum(table_part, ("seq", "ctx", "fsdp"))
    folded = fold_rows(grad_down.reshape(shards, -1, features), features // shards)
    parts = [
        grad_self_projections,
        grad_self_output,
        grad_cross_query,
        grad_cross_both,
        grad_cross_output,
        grad_gate,
        grad_linear,
        folded.reshape(features, width),
        gain_columns((grad_self_gain, grad_cross_gain, grad_feed_gain), jnp.bfloat16),
    ]
    terms = even_columns([member.astype(jnp.bfloat16) for member in parts])
    summed = reduce_terms(terms).astype(jnp.float32)
    squares = [summed[:, number * features : (number + 1) * features] for number in range(8)]
    first = 8 * features
    down_first = first + 2 * hidden
    gain_first = down_first + width
    return (
        layer_out[None],
        input_grad[None],
        encoder_grad[None],
        grad_table,
        summed[:, gain_first],
        squares[0],
        squares[1],
        squares[2],
        squares[3],
        summed[:, gain_first + 1],
        squares[4],
        squares[5],
        squares[6],
        squares[7],
        summed[:, gain_first + 2],
        summed[:, first : first + hidden],
        summed[:, first + hidden : down_first],
        unfold_rows(summed[:, down_first:gain_first], hidden // shards, features),
    )


def solution(mesh):
    return jax.shard_map(
        per_device,
        mesh=mesh,
        in_specs=(
            P(("seq", "fsdp"), "ctx", None),
            P(("seq", "fsdp"), "ctx", None),
            P(("seq", "fsdp"), "ctx", None),
            P(),
            P(),
            P(("ctx", "fsdp")),
            P(("ctx", "fsdp"), None),
            P(("ctx", "fsdp"), None),
            P(("ctx", "fsdp"), None),
            P(("ctx", "fsdp"), None),
            P(("ctx", "fsdp")),
            P(("ctx", "fsdp"), None),
            P(("ctx", "fsdp"), None),
            P(("ctx", "fsdp"), None),
            P(("ctx", "fsdp"), None),
            P(("ctx", "fsdp")),
            P(("ctx", "fsdp"), None),
            P(("ctx", "fsdp"), None),
            P(("ctx", "fsdp"), None),
        ),
        out_specs=(
            P(("seq", "fsdp"), "ctx", None),
            P(("seq", "fsdp"), "ctx", None),
            P(("seq", "fsdp"), "ctx", None),
            P(),
            P(("ctx", "fsdp")),
            P(("ctx", "fsdp"), None),
            P(("ctx", "fsdp"), None),
            P(("ctx", "fsdp"), None),
            P(("ctx", "fsdp"), None),
            P(("ctx", "fsdp")),
            P(("ctx", "fsdp"), None),
            P(("ctx", "fsdp"), None),
            P(("ctx", "fsdp"), None),
            P(("ctx", "fsdp"), None),
            P(("ctx", "fsdp")),
            P(("ctx", "fsdp"), None),
            P(("ctx", "fsdp"), None),
            P(("ctx", "fsdp"), None),
        ),
        check_vma=False,
    )
```

```python
from functools import partial
import math

import jax
import jax.numpy as jnp
from jax import lax
from jax.sharding import PartitionSpec as P

EPSILON = 1e-06
NEGATIVE = -1e30
HIGHEST = lax.Precision.HIGHEST


LANES = 128


def fold_rows(rows, height):
    count = -(-rows.shape[-2] // height)
    short = count * height - rows.shape[-2]
    padding = [(0, 0)] * (rows.ndim - 2) + [(0, short), (0, 0)]
    padded = jnp.pad(rows, padding)
    return jnp.concatenate(
        [padded[..., number * height : (number + 1) * height, :] for number in range(count)],
        axis=-1,
    )


def unfold_rows(columns, row_count, features):
    count = columns.shape[-1] // features
    stacked = jnp.concatenate(
        [columns[..., number * features : (number + 1) * features] for number in range(count)],
        axis=-2,
    )
    return stacked[..., :row_count, :]


def gain_columns(gains, dtype):
    columns = jnp.stack([member.astype(dtype) for member in gains], axis=1)
    return jnp.pad(columns, ((0, 0), (0, LANES - columns.shape[1])))


def product(left, right):
    return jnp.dot(left, right, preferred_element_type=jnp.float32)


def row_contract(left, right):
    return lax.dot_general(
        left, right, (((0,), (0,)), ((), ())), preferred_element_type=jnp.float32
    )


def col_contract(left, right):
    return lax.dot_general(
        left, right, (((1,), (1,)), ((), ())), preferred_element_type=jnp.float32
    )


def norm_forward(values, gain):
    inverse = lax.rsqrt(jnp.mean(values * values, axis=-1, keepdims=True) + EPSILON)
    normed = values * inverse
    return ((normed * gain.astype(jnp.float32)).astype(jnp.bfloat16), normed, inverse)


def norm_backward(upstream, normed, inverse, gain):
    grad_gain = jnp.sum(upstream * normed, axis=0)
    grad_normed = upstream * gain.astype(jnp.float32)
    grad_values = inverse * (
        grad_normed - normed * jnp.mean(grad_normed * normed, axis=-1, keepdims=True)
    )
    return (grad_values, grad_gain)


def geglu(gate_pre, linear_pre):
    return jax.nn.gelu(gate_pre, approximate=True) * linear_pre


def by_heads(values, head_count):
    return values.reshape(values.shape[0], head_count, values.shape[1] // head_count)


def band_onehot(bucket_rev, buckets, query_rows, key_rows, query_first, key_first):
    length = bucket_rev.shape[0] // 2
    offset_first = query_first - key_first
    upper_band = lax.dynamic_slice_in_dim(bucket_rev, length - 1 - offset_first, key_rows, 0)
    lower_band = lax.dynamic_slice_in_dim(
        bucket_rev, length - offset_first - query_rows, query_rows - 1, 0
    )
    slots = jnp.concatenate([upper_band, jnp.full((1,), -1, jnp.int32), lower_band])
    return (slots[:, None] == jnp.arange(buckets, dtype=jnp.int32)[None, :]).astype(jnp.float32)


def spread_band(band, query_rows, key_rows):
    head_count, width = band.shape
    tiled = jnp.broadcast_to(band[:, None, :], (head_count, query_rows, width)).reshape(
        head_count, query_rows * width
    )
    return tiled[:, : query_rows * (width - 1)].reshape(head_count, query_rows, width - 1)[
        :, :, :key_rows
    ]


def fold_band(grad_scores, width):
    head_count, query_rows, key_rows = grad_scores.shape
    padded = jnp.pad(grad_scores, ((0, 0), (0, 0), (0, width - 1 - key_rows))).reshape(
        head_count, query_rows * (width - 1)
    )
    padded = jnp.pad(padded, ((0, 0), (0, query_rows)))
    return jnp.sum(padded.reshape(head_count, query_rows, width), axis=1)


def self_scores(query, key_block, query_first, key_first, bucket_rev, bias_table):
    head_count = bias_table.shape[1]
    query_rows = query.shape[0]
    key_rows = key_block.shape[0]
    scores = jnp.einsum(
        "qhe,khe->hqk",
        by_heads(query, head_count),
        by_heads(key_block, head_count),
        preferred_element_type=jnp.float32,
    )
    offset = (query_first + jnp.arange(query_rows, dtype=jnp.int32))[:, None] - (
        key_first + jnp.arange(key_rows, dtype=jnp.int32)
    )[None, :]
    allowed = offset >= 0
    onehot = band_onehot(
        bucket_rev, bias_table.shape[0], query_rows, key_rows, query_first, key_first
    )
    band = jnp.dot(onehot, bias_table, precision=HIGHEST).T
    scores = jnp.where(allowed[None], scores + spread_band(band, query_rows, key_rows), NEGATIVE)
    return (scores, allowed, onehot)


def table_terms(grad_scores, onehot):
    band_grad = fold_band(grad_scores, onehot.shape[0])
    return jnp.dot(onehot.T, band_grad.T, precision=HIGHEST)


def fold_blocks(block_step, running, arrays, first_row):
    piece_rows = arrays[0].shape[0]
    block_size = math.gcd(piece_rows, 512) if piece_rows > 512 else piece_rows
    if block_size == piece_rows:
        return block_step(running, arrays, first_row)
    block_count = piece_rows // block_size
    stacked = tuple(
        (member.reshape((block_count, block_size) + member.shape[1:]) for member in arrays)
    )

    def scan_block(state_now, scanned):
        number, blocks = scanned
        return (block_step(state_now, blocks, first_row + number * block_size), None)

    result, _ = lax.scan(scan_block, running, (jnp.arange(block_count, dtype=jnp.int32), stacked))
    return result


def forward_step(running, blocks, key_first, query, query_first, bucket_rev, bias_table):
    top, total, mixed = running
    key_block, value_block = blocks
    head_count = bias_table.shape[1]
    scores, allowed, _ = self_scores(
        query, key_block, query_first, key_first, bucket_rev, bias_table
    )
    new_top = jnp.maximum(top, jnp.max(scores, axis=-1))
    weights = jnp.where(allowed[None], jnp.exp(scores - new_top[:, :, None]), 0.0)
    rescale = jnp.exp(top - new_top)
    total = total * rescale + jnp.sum(weights, axis=-1)
    update = jnp.einsum(
        "hqk,khe->qhe",
        weights.astype(jnp.bfloat16),
        by_heads(value_block, head_count),
        preferred_element_type=jnp.float32,
    )
    mixed = mixed * rescale.T[:, :, None] + update
    return (new_top, total, mixed)


def backward_core(
    query,
    grad_attn,
    lse_rows,
    delta_rows,
    key_block,
    value_block,
    query_first,
    key_first,
    bucket_rev,
    bias_table,
):
    head_count = bias_table.shape[1]
    scores, allowed, onehot = self_scores(
        query, key_block, query_first, key_first, bucket_rev, bias_table
    )
    probs = jnp.where(allowed[None], jnp.exp(scores - lse_rows.T[:, :, None]), 0.0)
    grad_probs = jnp.einsum(
        "qhe,khe->hqk",
        by_heads(grad_attn, head_count),
        by_heads(value_block, head_count),
        preferred_element_type=jnp.float32,
    )
    grad_scores = probs * (grad_probs - delta_rows.T[:, :, None])
    return (probs, grad_scores, onehot)


def partial_step(
    running,
    blocks,
    key_first,
    query,
    grad_attn,
    lse_rows,
    delta_rows,
    query_first,
    bucket_rev,
    bias_table,
):
    grad_query, grad_keys, grad_values, table_part = running
    key_block, value_block = blocks
    head_count = bias_table.shape[1]
    probs, grad_scores, onehot = backward_core(
        query,
        grad_attn,
        lse_rows,
        delta_rows,
        key_block,
        value_block,
        query_first,
        key_first,
        bucket_rev,
        bias_table,
    )
    rounded = grad_scores.astype(jnp.bfloat16)
    grad_query = grad_query + jnp.einsum(
        "hqk,khe->qhe", rounded, by_heads(key_block, head_count), preferred_element_type=jnp.float32
    )
    key_part = jnp.einsum(
        "hqk,qhe->khe", rounded, by_heads(query, head_count), preferred_element_type=jnp.float32
    ).reshape(key_block.shape[0], -1)
    value_part = jnp.einsum(
        "hqk,qhe->khe",
        probs.astype(jnp.bfloat16),
        by_heads(grad_attn, head_count),
        preferred_element_type=jnp.float32,
    ).reshape(key_block.shape[0], -1)
    grad_keys = lax.dynamic_update_slice_in_dim(grad_keys, key_part, key_first, 0)
    grad_values = lax.dynamic_update_slice_in_dim(grad_values, value_part, key_first, 0)
    table_part = table_part + table_terms(grad_scores, onehot)
    return (grad_query, grad_keys, grad_values, table_part)


def plain_forward(query, keys, values, head_count):
    scores = jnp.einsum(
        "qhe,khe->hqk",
        by_heads(query, head_count),
        by_heads(keys, head_count),
        preferred_element_type=jnp.float32,
    )
    top = jnp.max(scores, axis=-1, keepdims=True)
    weights = jnp.exp(scores - top)
    total = jnp.sum(weights, axis=-1, keepdims=True)
    mixed = jnp.einsum(
        "hqk,khe->qhe",
        weights.astype(jnp.bfloat16),
        by_heads(values, head_count),
        preferred_element_type=jnp.float32,
    )
    result = (
        (mixed / jnp.transpose(total, (1, 0, 2))).reshape(query.shape[0], -1).astype(jnp.bfloat16)
    )
    return (result, (top + jnp.log(total))[:, :, 0])


def plain_backward(query, keys, values, lse, output, grad_output, head_count):
    split_grad = by_heads(grad_output, head_count)
    delta = jnp.sum(
        split_grad.astype(jnp.float32) * by_heads(output, head_count).astype(jnp.float32), axis=-1
    ).T
    scores = jnp.einsum(
        "qhe,khe->hqk",
        by_heads(query, head_count),
        by_heads(keys, head_count),
        preferred_element_type=jnp.float32,
    )
    probs = jnp.exp(scores - lse[:, :, None])
    grad_probs = jnp.einsum(
        "qhe,khe->hqk", split_grad, by_heads(values, head_count), preferred_element_type=jnp.float32
    )
    rounded = (probs * (grad_probs - delta[:, :, None])).astype(jnp.bfloat16)
    grad_query = jnp.einsum(
        "hqk,khe->qhe", rounded, by_heads(keys, head_count), preferred_element_type=jnp.float32
    ).reshape(query.shape[0], -1)
    grad_keys = jnp.einsum(
        "hqk,qhe->khe", rounded, by_heads(query, head_count), preferred_element_type=jnp.float32
    ).reshape(keys.shape[0], -1)
    grad_values = jnp.einsum(
        "hqk,qhe->khe", probs.astype(jnp.bfloat16), split_grad, preferred_element_type=jnp.float32
    ).reshape(keys.shape[0], -1)
    return (grad_query, grad_keys, grad_values)


def reduce_terms(terms, table_terms):
    groups = lax.axis_size("seq")
    share = terms.shape[1] // groups
    stacked = jnp.stack(
        [terms[:, number * share : (number + 1) * share] for number in range(groups)]
    )
    part = lax.psum_scatter(stacked, "seq", scatter_dimension=0, tiled=False)
    table = lax.psum(table_terms, ("seq", "ctx", "fsdp"))
    part, table = lax.optimization_barrier((part, table))
    part = lax.psum_scatter(part, ("ctx", "fsdp"), scatter_dimension=0, tiled=True)
    return join_columns(lax.all_gather(part, "seq", axis=0, tiled=False)), table


def join_columns(stacked):
    return jnp.concatenate([stacked[number] for number in range(stacked.shape[0])], axis=1)


def gather_pack(pack):
    share = pack.shape[1] // lax.axis_size("seq")
    own = lax.dynamic_slice_in_dim(pack, lax.axis_index("seq") * share, share, 1)
    rows = lax.all_gather(own, ("ctx", "fsdp"), axis=0, tiled=True)
    return join_columns(lax.all_gather(rows, "seq", axis=0, tiled=False))


def even_columns(members):
    joined = jnp.concatenate(members, axis=1)
    return jnp.pad(joined, ((0, 0), (0, -joined.shape[1] % (LANES * lax.axis_size("seq")))))


def per_device(
    hidden_in,
    encoder_states,
    out_grad,
    bucket_index,
    bias_table,
    self_gain,
    self_query,
    self_key,
    self_value,
    self_output,
    cross_gain,
    cross_query,
    cross_key,
    cross_value,
    cross_output,
    feed_gain,
    gate_weight,
    linear_weight,
    down_weight,
):
    shards = lax.axis_size(("ctx", "fsdp"))
    features = self_query.shape[1]
    hidden = gate_weight.shape[1]
    pack = even_columns(
        [
            self_query,
            self_key,
            self_value,
            self_output,
            cross_query,
            cross_key,
            cross_value,
            cross_output,
            gate_weight,
            linear_weight,
            fold_rows(down_weight, self_query.shape[0]),
            gain_columns((self_gain, cross_gain, feed_gain), jnp.bfloat16),
        ]
    )
    pack = gather_pack(pack)
    (
        self_query,
        self_key,
        self_value,
        self_output,
        cross_query,
        cross_key,
        cross_value,
        cross_output,
    ) = (pack[:, number * features : (number + 1) * features] for number in range(8))
    first = 8 * features
    gate_weight = pack[:, first : first + hidden]
    linear_weight = pack[:, first + hidden : first + 2 * hidden]
    first = first + 2 * hidden
    width = -(-(hidden // shards) // (features // shards)) * features
    down_weight = unfold_rows(
        pack[:, first : first + width].reshape(shards, -1, width), hidden // shards, features
    ).reshape(hidden, features)
    gains = pack[:, first + width : first + width + LANES].T
    self_gain, cross_gain, feed_gain = gains[0], gains[1], gains[2]
    tokens = hidden_in.shape[1]
    length = bucket_index.shape[0]
    head_count = bias_table.shape[1]
    buckets = bias_table.shape[0]
    query_first = lax.axis_index("ctx") * tokens
    bucket_rev = jnp.flip(jnp.concatenate([jnp.full((length,), -1, jnp.int32), bucket_index]))
    start_x = hidden_in[0].astype(jnp.float32)
    norm_one, normed_one, inverse_one = norm_forward(start_x, self_gain)
    projected = product(norm_one, pack[:, : 3 * features]).astype(jnp.bfloat16)
    query = projected[:, :features]
    encoder_local = encoder_states[0]
    cross_local = product(encoder_local, pack[:, 5 * features : 7 * features]).astype(jnp.bfloat16)
    encoder_rows = encoder_local.shape[0]
    blocks = lax.all_gather(
        jnp.concatenate([projected[:, features:], cross_local], axis=0), "ctx", axis=0, tiled=False
    )
    both = blocks[:, :tokens].reshape(length, 2 * features)
    keys, values = both[:, :features], both[:, features:]
    both = blocks[:, tokens:].reshape(-1, 2 * features)
    cross_keys, cross_values = both[:, :features], both[:, features:]
    empty_top = jnp.full((head_count, tokens), NEGATIVE, jnp.float32)
    empty_total = jnp.zeros((head_count, tokens), jnp.float32)
    empty_mixed = jnp.zeros((tokens, head_count, query.shape[1] // head_count), jnp.float32)
    forward_bound = partial(
        forward_step,
        query=query,
        query_first=query_first,
        bucket_rev=bucket_rev,
        bias_table=bias_table,
    )
    top, total, mixed = fold_blocks(
        forward_bound,
        (empty_top, empty_total, empty_mixed),
        (keys, values),
        jnp.int32(0),
    )
    attn = (mixed / total.T[:, :, None]).reshape(tokens, -1).astype(jnp.bfloat16)
    self_lse = (top + jnp.log(total)).T
    after_self = start_x + product(attn, self_output)
    norm_two, normed_two, inverse_two = norm_forward(after_self, cross_gain)
    cross_q = product(norm_two, cross_query).astype(jnp.bfloat16)
    cattn, cross_lse = plain_forward(cross_q, cross_keys, cross_values, head_count)
    after_cross = after_self + product(cattn, cross_output)
    norm_three, normed_three, inverse_three = norm_forward(after_cross, feed_gain)
    gate_pre = product(norm_three, gate_weight)
    linear_pre = product(norm_three, linear_weight)
    middle = geglu(gate_pre, linear_pre).astype(jnp.bfloat16)
    layer_out = (after_cross + product(middle, down_weight)).astype(jnp.bfloat16)
    grad_top = out_grad[0]
    grad_down = row_contract(middle, grad_top)
    grad_middle = col_contract(grad_top, down_weight)
    _, pull_back = jax.vjp(geglu, gate_pre, linear_pre)
    grad_gate_pre, grad_linear_pre = pull_back(grad_middle)
    gate_round = grad_gate_pre.astype(jnp.bfloat16)
    linear_round = grad_linear_pre.astype(jnp.bfloat16)
    grad_gate = row_contract(norm_three, gate_round)
    grad_linear = row_contract(norm_three, linear_round)
    back_three, grad_feed_gain = norm_backward(
        col_contract(gate_round, gate_weight) + col_contract(linear_round, linear_weight),
        normed_three,
        inverse_three,
        feed_gain,
    )
    grad_after_cross = grad_top.astype(jnp.float32) + back_three
    cross_round = grad_after_cross.astype(jnp.bfloat16)
    grad_cross_output = row_contract(cattn, cross_round)
    grad_cattn = col_contract(cross_round, cross_output).astype(jnp.bfloat16)
    grad_cq, cross_key_terms, cross_value_terms = plain_backward(
        cross_q, cross_keys, cross_values, cross_lse, cattn, grad_cattn, head_count
    )
    grad_cq = grad_cq.astype(jnp.bfloat16)
    grad_cross_query = row_contract(norm_two, grad_cq)
    back_two, grad_cross_gain = norm_backward(
        col_contract(grad_cq, cross_query), normed_two, inverse_two, cross_gain
    )
    grad_after_self = grad_after_cross + back_two
    self_round = grad_after_self.astype(jnp.bfloat16)
    grad_self_output = row_contract(attn, self_round)
    grad_attn = col_contract(self_round, self_output).astype(jnp.bfloat16)
    delta_rows = jnp.sum(
        by_heads(grad_attn, head_count).astype(jnp.float32)
        * by_heads(attn, head_count).astype(jnp.float32),
        axis=-1,
    )
    empty_rows = jnp.zeros((tokens, query.shape[1]), jnp.float32)
    empty_table = jnp.zeros((buckets, head_count), jnp.float32)
    partial_bound = partial(
        partial_step,
        query=query,
        grad_attn=grad_attn,
        lse_rows=self_lse,
        delta_rows=delta_rows,
        query_first=query_first,
        bucket_rev=bucket_rev,
        bias_table=bias_table,
    )
    empty_whole = jnp.zeros((length, query.shape[1]), jnp.float32)
    grad_query, key_terms, value_terms, table_part = fold_blocks(
        partial_bound,
        (empty_rows.reshape(tokens, head_count, -1), empty_whole, empty_whole, empty_table),
        (keys, values),
        jnp.int32(0),
    )
    terms = jnp.concatenate(
        [
            jnp.concatenate([key_terms, value_terms], axis=1).reshape(-1, tokens, 2 * features),
            jnp.concatenate([cross_key_terms, cross_value_terms], axis=1).reshape(
                -1, encoder_rows, 2 * features
            ),
        ],
        axis=1,
    ).astype(jnp.bfloat16)
    sums = lax.psum_scatter(terms, "ctx", scatter_dimension=0, tiled=False)
    cross_both = sums[tokens:]
    grad_cross_both = row_contract(encoder_local, cross_both)
    grad_cross_key, grad_cross_value = (
        grad_cross_both[:, :features],
        grad_cross_both[:, features:],
    )
    encoder_grad = col_contract(cross_both, pack[:, 5 * features : 7 * features])
    grad_q = grad_query.reshape(tokens, -1).astype(jnp.bfloat16)
    grad_projected = jnp.concatenate([grad_q, sums[:tokens]], axis=1)
    grad_self_projections = row_contract(norm_one, grad_projected)
    upstream_one = col_contract(grad_projected, pack[:, : 3 * features])
    back_one, grad_self_gain = norm_backward(upstream_one, normed_one, inverse_one, self_gain)
    input_grad = grad_after_self + back_one
    folded = fold_rows(grad_down.reshape(shards, -1, features), features // shards)
    parts = [
        grad_self_projections,
        grad_self_output,
        grad_cross_query,
        grad_cross_both,
        grad_cross_output,
        grad_gate,
        grad_linear,
        folded.reshape(features, width),
        gain_columns((grad_self_gain, grad_cross_gain, grad_feed_gain), jnp.bfloat16),
    ]
    terms = even_columns([member.astype(jnp.bfloat16) for member in parts])
    summed, grad_table = reduce_terms(terms, table_part)
    summed = summed.astype(jnp.float32)
    squares = [summed[:, number * features : (number + 1) * features] for number in range(8)]
    first = 8 * features
    down_first = first + 2 * hidden
    gain_first = down_first + width
    return (
        layer_out[None],
        input_grad[None],
        encoder_grad[None],
        grad_table,
        summed[:, gain_first],
        squares[0],
        squares[1],
        squares[2],
        squares[3],
        summed[:, gain_first + 1],
        squares[4],
        squares[5],
        squares[6],
        squares[7],
        summed[:, gain_first + 2],
        summed[:, first : first + hidden],
        summed[:, first + hidden : down_first],
        unfold_rows(summed[:, down_first:gain_first], hidden // shards, features),
    )


def solution(mesh):
    return jax.shard_map(
        per_device,
        mesh=mesh,
        in_specs=(
            P(("seq", "fsdp"), "ctx", None),
            P(("seq", "fsdp"), "ctx", None),
            P(("seq", "fsdp"), "ctx", None),
            P(),
            P(),
            P(("ctx", "fsdp")),
            P(("ctx", "fsdp"), None),
            P(("ctx", "fsdp"), None),
            P(("ctx", "fsdp"), None),
            P(("ctx", "fsdp"), None),
            P(("ctx", "fsdp")),
            P(("ctx", "fsdp"), None),
            P(("ctx", "fsdp"), None),
            P(("ctx", "fsdp"), None),
            P(("ctx", "fsdp"), None),
            P(("ctx", "fsdp")),
            P(("ctx", "fsdp"), None),
            P(("ctx", "fsdp"), None),
            P(("ctx", "fsdp"), None),
        ),
        out_specs=(
            P(("seq", "fsdp"), "ctx", None),
            P(("seq", "fsdp"), "ctx", None),
            P(("seq", "fsdp"), "ctx", None),
            P(),
            P(("ctx", "fsdp")),
            P(("ctx", "fsdp"), None),
            P(("ctx", "fsdp"), None),
            P(("ctx", "fsdp"), None),
            P(("ctx", "fsdp"), None),
            P(("ctx", "fsdp")),
            P(("ctx", "fsdp"), None),
            P(("ctx", "fsdp"), None),
            P(("ctx", "fsdp"), None),
            P(("ctx", "fsdp"), None),
            P(("ctx", "fsdp")),
            P(("ctx", "fsdp"), None),
            P(("ctx", "fsdp"), None),
            P(("ctx", "fsdp"), None),
        ),
        check_vma=False,
    )
```
